32 devices in a mesh: fsdp: 8 (over z, x), rep: 4 (over y, core).
Axes of the slice: x: 2, y: 2, z: 4, core: 2. Of those that a mesh axis runs over, the one named last changes fastest.
Arguments:
- samples: bfloat16 [768, 4096], P(('fsdp', 'rep')), may hold values from -10 to 10
- dual_weight: bfloat16 [8192, 4096], P('fsdp'), may hold values from -0.09375 to 0.09375
- dual_vector: float32 [2, 8192], P(None, 'fsdp'), may hold values from 0 to 2
- map_weight: float32 [8192, 4096], P(('fsdp', 'rep')), may hold values from -0.09375 to 0.09375
- map_vector: float32 [2, 8192], P(None, ('fsdp', 'rep')), may hold values from 0.001 to 2
- moment_weight: float32 [8192, 4096], P(('fsdp', 'rep')), may hold values from -0.006 to 0.006
- square_weight: float32 [8192, 4096], P(('fsdp', 'rep')), may hold values from 0.0001 to 0.01
- moment_vector: float32 [2, 8192], P(None, ('fsdp', 'rep')), may hold values from -0.03 to 0.03
- square_vector: float32 [2, 8192], P(None, ('fsdp', 'rep')), may hold values from 0.0001 to 0.01
Outputs:
- next_weight: float32 [8192, 4096], P(('fsdp', 'rep'))
- next_vector: float32 [2, 8192], P(None, ('fsdp', 'rep'))
- next_moment_weight: float32 [8192, 4096], P(('fsdp', 'rep'))
- next_square_weight: float32 [8192, 4096], P(('fsdp', 'rep'))
- next_moment_vector: float32 [2, 8192], P(None, ('fsdp', 'rep'))
- next_square_vector: float32 [2, 8192], P(None, ('fsdp', 'rep'))
The draws below stay inside these ranges and needn't reach their ends.
All inputs are finite; a program needn't handle non-finite values.
Results may differ from the reference program's by a relative error of at most 0.004.
Values may be sent and summed in bfloat16 or wider, within the bound.
A program may use at most 128 MiB of HBM per device.

```python
import math
import jax
import jax.numpy as jnp
from jax import lax

D = 4096
H = 8192
ROWS = 768
N_FSDP = 8


def draw_samples(key, part):
    base_key = jax.random.fold_in(key, 11)
    scale_key = jax.random.fold_in(key, 12)
    base = jax.random.truncated_normal(base_key, -4.0, 4.0, (ROWS, D), jnp.float32)
    row_scale = jnp.exp(jax.random.uniform(scale_key, (ROWS, 1), jnp.float32, math.log(0.25), math.log(2.5)))
    return (base * row_scale).astype(jnp.bfloat16)


def steps_of(own_key, dims, cuts, least, high):
    factor_of, own = 1.0, jax.random.fold_in(own_key, 6)
    for dim, shards_of in cuts:
        heights = jnp.exp(jax.random.uniform(jax.random.fold_in(own, dim), (shards_of,), jnp.float32, least / len(cuts), high / len(cuts)))
        factor_of = factor_of * jnp.repeat(heights, dims[dim] // shards_of).reshape([-1 if axis == dim else 1 for axis in range(len(dims))])
    return factor_of


def centred(own_key, shape, deviation, bound, split=(), dtype=jnp.bfloat16):
    values = deviation * jax.random.normal(own_key, shape, jnp.float32)
    if split:
        values = values * steps_of(own_key, shape, split, -0.22, 0.18)
    return jnp.clip(values, -bound, bound).astype(dtype)


def setup_inputs(seed: int = 0) -> dict:
    streams_of = jax.random.split(jax.random.key(seed), 10)
    samples = draw_samples(jax.random.fold_in(streams_of[9], 71), 0)
    dual_weight = centred(streams_of[1], (H, D), D ** -0.5, 0.09375, ((0, 8),))
    dual_vector = jnp.clip(2.0 * jax.random.uniform(streams_of[2], (2, H), jnp.float32) ** steps_of(streams_of[2], (2, H), ((1, 8),), -0.2, 0.2), 0.0, 2.0)
    map_weight = centred(streams_of[3], (H, D), D ** -0.5, 0.09375, ((0, 32),), jnp.float32)
    map_vector = jnp.clip(jnp.exp(math.log(2.0) - 7.6009024 * jax.random.uniform(streams_of[4], (2, H), jnp.float32) ** steps_of(streams_of[4], (2, H), ((1, 32),), -0.2, 0.2)), 0.001, 2.0)
    moment_weight = centred(streams_of[5], (H, D), 0.001, 0.006, ((0, 32),), jnp.float32)
    square_weight = jnp.clip(jnp.exp(math.log(0.01) - 4.6051702 * jax.random.uniform(streams_of[6], (H, D), jnp.float32) ** steps_of(streams_of[6], (H, D), ((0, 32),), -0.2, 0.2)), 0.0001, 0.01)
    moment_vector = centred(streams_of[7], (2, H), 0.005, 0.03, ((1, 32),), jnp.float32)
    square_vector = jnp.clip(jnp.exp(math.log(0.01) - 4.6051702 * jax.random.uniform(streams_of[8], (2, H), jnp.float32) ** steps_of(streams_of[8], (2, H), ((1, 32),), -0.2, 0.2)), 0.0001, 0.01)
    return dict(samples=samples, dual_weight=dual_weight, dual_vector=dual_vector, map_weight=map_weight, map_vector=map_vector, moment_weight=moment_weight, square_weight=square_weight, moment_vector=moment_vector, square_vector=square_vector)


beta_one = 0.9
beta_two = 0.999
learn_rate = 0.001
epsilon = 1e-08
adam_step = 10

def contract_last(left, right):
    return lax.dot_general(left, right, (((1,), (1,)), ((), ())), preferred_element_type=jnp.float32)

def contract_first(left, right):
    return lax.dot_general(left, right, (((0,), (0,)), ((), ())), preferred_element_type=jnp.float32)

def block_sum(left, right):
    block_size = right.shape[0] // N_FSDP
    left_blocks = jnp.transpose(left.reshape(left.shape[0], N_FSDP, block_size), (1, 0, 2))
    right_blocks = right.reshape(N_FSDP, block_size, right.shape[1])

    def add_block(running, pieces):
        partial_sum = jnp.dot(pieces[0], pieces[1], preferred_element_type=jnp.float32)
        rounded = lax.optimization_barrier(partial_sum.astype(jnp.bfloat16)).astype(jnp.float32)
        return (running + rounded, None)
    initial = jnp.zeros((left.shape[0], right.shape[1]), jnp.float32)
    running, _ = lax.scan(add_block, initial, (left_blocks, right_blocks))
    return running

def adam_update(param, grad, moment, square):
    moment_new = beta_one * moment + (1.0 - beta_one) * grad
    square_new = beta_two * square + (1.0 - beta_two) * grad * grad
    fix_one = 1.0 - beta_one ** adam_step
    fix_two = 1.0 - beta_two ** adam_step
    update = learn_rate * (moment_new / fix_one) / (jnp.sqrt(square_new / fix_two) + epsilon)
    return (param - update, moment_new, square_new)

def reference(samples, dual_weight, dual_vector, map_weight, map_vector, moment_weight, square_weight, moment_vector, square_vector):
    weight_low = map_weight.astype(jnp.bfloat16)
    vector_low = lax.optimization_barrier(map_vector.astype(jnp.bfloat16)).astype(jnp.float32)
    readout = vector_low[0]
    offset = vector_low[1]
    sample_float = samples.astype(jnp.float32)
    hidden = contract_last(samples, weight_low) + offset
    sigma = jax.nn.sigmoid(hidden)
    scaled = (readout * sigma).astype(jnp.bfloat16)
    mapped = sample_float + block_sum(scaled, weight_low)
    mapped_low = mapped.astype(jnp.bfloat16)
    dual_hidden = contract_last(mapped_low, dual_weight) + dual_vector[1]
    dual_scaled = (dual_vector[0] * jax.nn.sigmoid(dual_hidden)).astype(jnp.bfloat16)
    dual_grad = mapped + block_sum(dual_scaled, dual_weight)
    residual = (sample_float - dual_grad).astype(jnp.bfloat16)
    pulled = contract_last(residual, weight_low)
    slope = sigma * (1.0 - sigma)
    curve_term = (readout * slope * pulled).astype(jnp.bfloat16)
    inverse_rows = 1.0 / ROWS
    grad_weight = (contract_first(scaled, residual) + contract_first(curve_term, samples)) * inverse_rows
    grad_vector = jnp.stack([lax.optimization_barrier(jnp.sum(sigma * pulled, axis=0)), lax.optimization_barrier(jnp.sum(readout * slope * pulled, axis=0))]) * inverse_rows
    next_weight, next_moment_weight, next_square_weight = adam_update(map_weight, grad_weight, moment_weight, square_weight)
    raw_vector, next_moment_vector, next_square_vector = adam_update(map_vector, grad_vector, moment_vector, square_vector)
    next_vector = jnp.concatenate([jnp.maximum(raw_vector[0:1], 0.0), raw_vector[1:2]], axis=0)
    return (next_weight, next_vector, next_moment_weight, next_square_weight, next_moment_vector, next_square_vector)
```

```python
import jax
import jax.numpy as jnp
from jax import lax
from jax.experimental import pallas as pl
from jax.experimental.pallas import tpu as pltpu
from jax.sharding import PartitionSpec as P

beta_one = 0.9
beta_two = 0.999
learn_rate = 0.001
epsilon = 1e-08
adam_step = 10


def contract_last(left, right):
    return lax.dot_general(
        left, right, (((1,), (1,)), ((), ())), preferred_element_type=jnp.float32
    )


def contract_first(left, right):
    return lax.dot_general(
        left, right, (((0,), (0,)), ((), ())), preferred_element_type=jnp.float32
    )


def adam_update(param, grad, moment, square):
    moment_new = beta_one * moment + (1.0 - beta_one) * grad
    square_new = beta_two * square + (1.0 - beta_two) * grad * grad
    fix_one = 1.0 - beta_one**adam_step
    fix_two = 1.0 - beta_two**adam_step
    update = learn_rate * (moment_new / fix_one) / (jnp.sqrt(square_new / fix_two) + epsilon)
    return (param - update, moment_new, square_new)


MESH = pl.DeviceIdType.MESH
F32 = jnp.float32
BF16 = jnp.bfloat16


def place():
    fsdp, rep = lax.axis_index("fsdp"), lax.axis_index("rep")
    z, x = fsdp // 2, fsdp % 2
    y, core = rep // 2, rep % 2
    z_peers = [(lax.rem(z + k, 4) * 2 + x, rep) for k in (1, 2, 3)]
    x_peer = (z * 2 + 1 - x, rep)
    y_peer = (fsdp, (1 - y) * 2 + core)
    return z, x, y, z_peers, x_peer, y_peer


def greet(peers):
    barrier = pltpu.get_barrier_semaphore()
    for peer in peers:
        pl.semaphore_signal(barrier, inc=1, device_id=peer, device_id_type=MESH)
    pl.semaphore_wait(barrier, len(peers))


class Sender:
    def __init__(self, send_sem, recv_sem):
        self.send_sem, self.recv_sem, self.copies = send_sem, recv_sem, []

    def send(self, src, dst, device):
        i = len(self.copies)
        copy = pltpu.make_async_remote_copy(
            src_ref=src,
            dst_ref=dst,
            send_sem=self.send_sem.at[i],
            recv_sem=self.recv_sem.at[i],
            device_id=device,
            device_id_type=MESH,
        )
        copy.start()
        self.copies.append(copy)
        return copy

    def drain(self):
        for copy in self.copies:
            copy.wait_send()


def gather_line(sender, view, z, x, y, z_peers, x_peer, y_peer, own):
    here = view(z, x, y)
    to_z = [sender.send(own, here, peer) for peer in z_peers]
    over_x, over_y = [sender.send(own, here, x_peer)], []
    if y_peer is not None:
        over_y.append(sender.send(own, here, y_peer))
    for k in (1, 3, 2):
        source = lax.rem(z + 4 - k, 4)
        to_z[k - 1].wait_recv()
        block = view(source, x, y)
        over_x.append(sender.send(block, block, x_peer))
        if y_peer is not None:
            over_y.append(sender.send(block, block, y_peer))
    return over_x, over_y


def gather_all(sender, view, half, z, x, y, z_peers, x_peer, y_peer, own):
    over_x, over_y = gather_line(sender, view, z, x, y, z_peers, x_peer, y_peer, own)
    diagonal = []
    for i, k in enumerate((0, 1, 3, 2)):
        source = lax.rem(z + 4 - k, 4)
        over_x[i].wait_recv()
        block = half(source, 1 - x, y, 0)
        diagonal.append(sender.send(block, block, y_peer))
        over_y[i].wait_recv()
        block = half(source, x, 1 - y, 1)
        diagonal.append(sender.send(block, block, x_peer))
    for copy in diagonal:
        copy.wait_recv()


def gather_kernel(own_ref, all_ref, send_sem, recv_sem, local_sem):
    z, x, y, z_peers, x_peer, y_peer = place()
    width = own_ref.shape[1] // 2
    view = lambda zz, xx, yy: all_ref.at[yy * 8 + zz * 2 + xx]
    half = lambda zz, xx, yy, h: all_ref.at[yy * 8 + zz * 2 + xx, :, pl.ds(h * width, width)]
    greet(z_peers + [x_peer, y_peer])
    local = pltpu.make_async_copy(own_ref, view(z, x, y), local_sem)
    local.start()
    sender = Sender(send_sem, recv_sem)
    gather_all(sender, view, half, z, x, y, z_peers, x_peer, y_peer, own_ref)
    sender.drain()
    local.wait()


def gather_samples(samples):
    rows, width = samples.shape
    gathered = pl.pallas_call(
        gather_kernel,
        out_shape=jax.ShapeDtypeStruct((16, rows, width), samples.dtype),
        in_specs=[pl.BlockSpec(memory_space=pl.ANY)],
        out_specs=pl.BlockSpec(memory_space=pl.ANY),
        scratch_shapes=[
            pltpu.SemaphoreType.DMA((19,)),
            pltpu.SemaphoreType.DMA((19,)),
            pltpu.SemaphoreType.DMA,
        ],
        compiler_params=pltpu.CompilerParams(collective_id=1, has_side_effects=True),
        cost_estimate=pl.CostEstimate(flops=0, bytes_accessed=100_000_000, transcendentals=0),
    )(samples)
    return gathered.reshape(16 * rows, width)


def map_kernel(
    part, base, mapped, low, from_y, from_x, to_x, to_y, late_x, late_y, to_z, from_z, send_sem, recv_sem
):
    z, x, y, z_peers, x_peer, y_peer = place()
    rows, width = base.shape
    half = rows // 2
    cols = lambda zz, xx: pl.ds(pl.multiple_of((zz * 2 + xx) * width, width), width)
    lines = lambda yy, h: pl.ds(pl.multiple_of(yy * rows + h * half, half), half)
    lane = lambda xx: pl.ds(pl.multiple_of(xx * width, width), width)
    greet(z_peers + [x_peer, y_peer])
    sender = Sender(send_sem, recv_sem)
    order = (2, 1, 3, 0)
    first_y, first_x = {}, {}
    for k in order:
        zz = lax.rem(z + k, 4)
        pair = pl.ds(pl.multiple_of(zz * 2 * width, 2 * width), 2 * width)
        first_y[k] = sender.send(part.at[lines(1 - y, 0), pair], from_y.at[k], y_peer)
        first_x[k] = [
            sender.send(part.at[lines(yy, 1), cols(zz, 1 - x)], from_x.at[k, yy], x_peer) for yy in (0, 1)
        ]
    second_x, second_y = {}, {}
    for k in order:
        zz = lax.rem(z + k, 4)
        first_y[k].wait_recv()
        to_x[k] = (
            part[lines(y, 0), cols(zz, 1 - x)].astype(F32) + from_y[k, :, lane(1 - x)].astype(F32)
        ).astype(BF16)
        second_x[k] = sender.send(to_x.at[k], late_x.at[k], x_peer)
        for copy in first_x[k]:
            copy.wait_recv()
        to_y[k] = (
            part[lines(1 - y, 1), cols(zz, x)].astype(F32) + from_x[k, 1 - y].astype(F32)
        ).astype(BF16)
        second_y[k] = sender.send(to_y.at[k], late_y.at[k], y_peer)
    third = {}
    for k in order:
        zz = lax.rem(z + k, 4)
        second_x[k].wait_recv()
        top = (
            part[lines(y, 0), cols(zz, x)].astype(F32)
            + from_y[k, :, lane(x)].astype(F32)
            + late_x[k].astype(F32)
        )
        second_y[k].wait_recv()
        bottom = (
            part[lines(y, 1), cols(zz, x)].astype(F32) + from_x[k, y].astype(F32) + late_y[k].astype(F32)
        )
        if k:
            to_z[k - 1, :half] = top.astype(BF16)
            to_z[k - 1, half:] = bottom.astype(BF16)
            third[k] = sender.send(to_z.at[k - 1], from_z.at[k - 1], z_peers[k - 1])
        else:
            mapped[:half] = top + base[:half].astype(F32)
            mapped[half:] = bottom + base[half:].astype(F32)
    for k in (1, 2, 3):
        third[k].wait_recv()
    total = mapped[...] + (from_z[0].astype(F32) + from_z[1].astype(F32) + from_z[2].astype(F32))
    mapped[...] = total
    low[:, cols(z, x)] = total.astype(BF16)
    view = lambda zz, xx, yy: low.at[:, cols(zz, xx)]
    over_x, _ = gather_line(sender, view, z, x, y, z_peers, x_peer, None, view(z, x, y))
    for copy in over_x:
        copy.wait_recv()
    sender.drain()


def reduce_map(part, base):
    rows, width = base.shape
    half = rows // 2
    return pl.pallas_call(
        map_kernel,
        out_shape=(
            jax.ShapeDtypeStruct((rows, width), F32),
            jax.ShapeDtypeStruct((rows, part.shape[1]), BF16),
        ),
        in_specs=[pl.BlockSpec(memory_space=pltpu.VMEM)] * 2,
        out_specs=[pl.BlockSpec(memory_space=pltpu.VMEM)] * 2,
        scratch_shapes=[
            pltpu.VMEM((4, half, 2 * width), BF16),
            pltpu.VMEM((4, 2, half, width), BF16),
            pltpu.VMEM((4, half, width), BF16),
            pltpu.VMEM((4, half, width), BF16),
            pltpu.VMEM((4, half, width), BF16),
            pltpu.VMEM((4, half, width), BF16),
            pltpu.VMEM((3, rows, width), BF16),
            pltpu.VMEM((3, rows, width), BF16),
            pltpu.SemaphoreType.DMA((30,)),
            pltpu.SemaphoreType.DMA((30,)),
        ],
        compiler_params=pltpu.CompilerParams(collective_id=2, has_side_effects=True),
    )(part, base)


def dual_kernel(part, base, mapped, pulled_from, from_x, to_z, from_z, kept, send_sem, recv_sem):
    z, x, y, z_peers, x_peer, y_peer = place()
    rows, width = base.shape
    half_rows = rows // 2
    cols = lambda zz, xx: pl.ds(pl.multiple_of((zz * 2 + xx) * width, width), width)
    greet(z_peers + [x_peer, y_peer])
    sender = Sender(send_sem, recv_sem)
    order = (2, 1, 3, 0)
    first, third = {}, {}
    for k in order:
        first[k] = sender.send(part.at[:, cols(lax.rem(z + k, 4), 1 - x)], from_x.at[k], x_peer)
    for k in order:
        first[k].wait_recv()
        total = part[:, cols(lax.rem(z + k, 4), x)].astype(F32) + from_x[k].astype(F32)
        if k:
            to_z[k - 1] = total.astype(BF16)
            third[k] = sender.send(to_z.at[k - 1], from_z.at[k - 1], z_peers[k - 1])
        else:
            kept[...] = mapped[...] + total
    for k in (1, 2, 3):
        third[k].wait_recv()
    grad = kept[...] + (from_z[0].astype(F32) + from_z[1].astype(F32) + from_z[2].astype(F32))
    view = lambda zz, xx, yy: pulled_from.at[pl.ds(pl.multiple_of(yy * rows, rows), rows), cols(zz, xx)]
    half = lambda zz, xx, yy, h: pulled_from.at[
        pl.ds(pl.multiple_of(yy * rows + h * half_rows, half_rows), half_rows), cols(zz, xx)
    ]
    pulled_from[pl.ds(pl.multiple_of(y * rows, rows), rows), cols(z, x)] = (
        base[...].astype(F32) - grad
    ).astype(BF16)
    gather_all(sender, view, half, z, x, y, z_peers, x_peer, y_peer, view(z, x, y))
    sender.drain()


def reduce_dual(part, base, mapped):
    rows, width = base.shape
    return pl.pallas_call(
        dual_kernel,
        out_shape=jax.ShapeDtypeStruct((2 * rows, part.shape[1]), BF16),
        in_specs=[pl.BlockSpec(memory_space=pltpu.VMEM)] * 3,
        out_specs=pl.BlockSpec(memory_space=pltpu.VMEM),
        scratch_shapes=[
            pltpu.VMEM((4, rows, width), BF16),
            pltpu.VMEM((3, rows, width), BF16),
            pltpu.VMEM((3, rows, width), BF16),
            pltpu.VMEM((rows, width), F32),
            pltpu.SemaphoreType.DMA((26,)),
            pltpu.SemaphoreType.DMA((26,)),
        ],
        compiler_params=pltpu.CompilerParams(collective_id=3, has_side_effects=True),
    )(part, base, mapped)


def chip_body(
    samples,
    dual_weight,
    dual_vector,
    map_weight,
    map_vector,
    moment_weight,
    square_weight,
    moment_vector,
    square_vector,
):
    swap = [(0, 1), (1, 0), (2, 3), (3, 2)]
    fsdp, rep = lax.axis_index("fsdp"), lax.axis_index("rep")
    weight = map_weight.astype(BF16)
    vector = map_vector.astype(BF16)
    weights = (weight, lax.ppermute(weight, "rep", swap))
    vectors = (vector, lax.ppermute(vector, "rep", swap))
    rows = gather_samples(samples)
    inverse_rows = 1.0 / (rows.shape[0] * 2)
    sigmas, scales = [], []
    for block, pair in zip(weights, vectors):
        sigma = jax.nn.sigmoid(contract_last(rows, block) + pair[1].astype(F32))
        sigmas.append(sigma)
        scales.append((pair[0].astype(F32) * sigma).astype(BF16))
    part = (
        jnp.dot(scales[0], weights[0], preferred_element_type=F32)
        + jnp.dot(scales[1], weights[1], preferred_element_type=F32)
    ).astype(BF16)
    half, width = rows.shape[0] // 2, rows.shape[1] // 8
    base = lax.dynamic_slice(rows, ((rep // 2) * half, fsdp * width), (half, width))
    mapped, mapped_low = reduce_map(part, base)
    dual_hidden = contract_last(mapped_low, dual_weight) + dual_vector[1]
    dual_scaled = (dual_vector[0] * jax.nn.sigmoid(dual_hidden)).astype(BF16)
    dual_part = jnp.dot(dual_scaled, dual_weight, preferred_element_type=F32).astype(BF16)
    residual = reduce_dual(dual_part, base, mapped)
    grads, smalls = [], []
    for block, pair, sigma, scaled in zip(weights[::-1], vectors[::-1], sigmas[::-1], scales[::-1]):
        readout = pair[0].astype(F32)
        pulled = contract_last(residual, block)
        curve = readout * (sigma * (1.0 - sigma)) * pulled
        grads.append(contract_first(scaled, residual) + contract_first(curve.astype(BF16), rows))
        smalls.append(jnp.stack([jnp.sum(sigma * pulled, axis=0), jnp.sum(curve, axis=0)]))
    owner_weight = (grads[1] + lax.ppermute(grads[0], "rep", swap)) * inverse_rows
    owner_vector = (smalls[1] + lax.ppermute(smalls[0], "rep", swap)) * inverse_rows
    next_weight, next_moment_weight, next_square_weight = adam_update(
        map_weight, owner_weight, moment_weight, square_weight
    )
    raw_vector, next_moment_vector, next_square_vector = adam_update(
        map_vector, owner_vector, moment_vector, square_vector
    )
    next_vector = jnp.concatenate([jnp.maximum(raw_vector[0:1], 0.0), raw_vector[1:2]], axis=0)
    return (
        next_weight,
        next_vector,
        next_moment_weight,
        next_square_weight,
        next_moment_vector,
        next_square_vector,
    )


def body(
    samples,
    dual_weight,
    dual_vector,
    map_weight,
    map_vector,
    moment_weight,
    square_weight,
    moment_vector,
    square_vector,
):
    group_rows = lax.all_gather(samples, "fsdp", axis=0, tiled=True)
    weight_slab, vector_slab = (
        lax.all_gather(map_weight.astype(jnp.bfloat16), "rep", axis=0, tiled=True),
        lax.all_gather(map_vector.astype(jnp.bfloat16), "rep", axis=1, tiled=True),
    )
    readout = vector_slab[0].astype(jnp.float32)
    offset = vector_slab[1].astype(jnp.float32)
    inverse_rows = 1.0 / (group_rows.shape[0] * lax.axis_size("rep"))
    hidden = contract_last(group_rows, weight_slab) + offset
    sigma = jax.nn.sigmoid(hidden)
    scaled = (readout * sigma).astype(jnp.bfloat16)
    group_float = group_rows.astype(jnp.float32)
    mapped = group_float + lax.psum(
        jnp.dot(scaled, weight_slab, preferred_element_type=jnp.float32).astype(jnp.bfloat16),
        "fsdp",
    ).astype(jnp.float32)
    mapped_low = mapped.astype(jnp.bfloat16)
    dual_hidden = contract_last(mapped_low, dual_weight) + dual_vector[1]
    dual_scaled = (dual_vector[0] * jax.nn.sigmoid(dual_hidden)).astype(jnp.bfloat16)
    dual_grad = mapped + lax.psum(
        jnp.dot(dual_scaled, dual_weight, preferred_element_type=jnp.float32).astype(jnp.bfloat16),
        "fsdp",
    ).astype(jnp.float32)
    residual = (group_float - dual_grad).astype(jnp.bfloat16)
    pulled = contract_last(residual, weight_slab)
    slope = sigma * (1.0 - sigma)
    curve_float = readout * slope * pulled
    curve_term = curve_float.astype(jnp.bfloat16)
    left_stack = jnp.concatenate([scaled, curve_term], axis=0)
    right_stack = jnp.concatenate([residual, group_rows], axis=0)
    grad_slab = contract_first(left_stack, right_stack) * inverse_rows
    grad_small = (
        jnp.stack([jnp.sum(sigma * pulled, axis=0), jnp.sum(curve_float, axis=0)]) * inverse_rows
    )
    owner_weight, owner_vector = (
        lax.psum_scatter(grad_slab, "rep", scatter_dimension=0, tiled=True),
        lax.psum_scatter(grad_small, "rep", scatter_dimension=1, tiled=True),
    )
    next_weight, next_moment_weight, next_square_weight = adam_update(
        map_weight, owner_weight, moment_weight, square_weight
    )
    raw_vector, next_moment_vector, next_square_vector = adam_update(
        map_vector, owner_vector, moment_vector, square_vector
    )
    next_vector = jnp.concatenate([jnp.maximum(raw_vector[0:1], 0.0), raw_vector[1:2]], axis=0)
    return (
        next_weight,
        next_vector,
        next_moment_weight,
        next_square_weight,
        next_moment_vector,
        next_square_vector,
    )


def solution(mesh):
    by_chip = mesh.shape["fsdp"] == 8 and mesh.shape["rep"] == 4
    return jax.shard_map(
        chip_body if by_chip else body,
        mesh=mesh,
        in_specs=(
            P(("fsdp", "rep"), None),
            P("fsdp", None),
            P(None, "fsdp"),
            P(("fsdp", "rep"), None),
            P(None, ("fsdp", "rep")),
            P(("fsdp", "rep"), None),
            P(("fsdp", "rep"), None),
            P(None, ("fsdp", "rep")),
            P(None, ("fsdp", "rep")),
        ),
        out_specs=(
            P(("fsdp", "rep"), None),
            P(None, ("fsdp", "rep")),
            P(("fsdp", "rep"), None),
            P(("fsdp", "rep"), None),
            P(None, ("fsdp", "rep")),
            P(None, ("fsdp", "rep")),
        ),
        check_vma=False,
    )
```

```python
import jax
import jax.numpy as jnp
from jax import lax
from jax.experimental import pallas as pl
from jax.experimental.pallas import tpu as pltpu
from jax.sharding import PartitionSpec as P

beta_one = 0.9
beta_two = 0.999
learn_rate = 0.001
epsilon = 1e-08
adam_step = 10


def contract_last(left, right):
    return lax.dot_general(
        left, right, (((1,), (1,)), ((), ())), preferred_element_type=jnp.float32
    )


def contract_first(left, right):
    return lax.dot_general(
        left, right, (((0,), (0,)), ((), ())), preferred_element_type=jnp.float32
    )


def adam_update(param, grad, moment, square):
    moment_new = beta_one * moment + (1.0 - beta_one) * grad
    square_new = beta_two * square + (1.0 - beta_two) * grad * grad
    fix_one = 1.0 - beta_one**adam_step
    fix_two = 1.0 - beta_two**adam_step
    update = learn_rate * (moment_new / fix_one) / (jnp.sqrt(square_new / fix_two) + epsilon)
    return (param - update, moment_new, square_new)


MESH = pl.DeviceIdType.MESH
F32 = jnp.float32
BF16 = jnp.bfloat16


def place():
    fsdp, rep = lax.axis_index("fsdp"), lax.axis_index("rep")
    z, x = fsdp // 2, fsdp % 2
    y, core = rep // 2, rep % 2
    z_peers = [(lax.rem(z + k, 4) * 2 + x, rep) for k in (1, 2, 3)]
    x_peer = (z * 2 + 1 - x, rep)
    y_peer = (fsdp, (1 - y) * 2 + core)
    return z, x, y, z_peers, x_peer, y_peer


def greet(peers):
    barrier = pltpu.get_barrier_semaphore()
    for peer in peers:
        pl.semaphore_signal(barrier, inc=1, device_id=peer, device_id_type=MESH)
    pl.semaphore_wait(barrier, len(peers))


class Sender:
    def __init__(self, send_sem, recv_sem):
        self.send_sem, self.recv_sem, self.copies = send_sem, recv_sem, []

    def send(self, src, dst, device):
        i = len(self.copies)
        copy = pltpu.make_async_remote_copy(
            src_ref=src,
            dst_ref=dst,
            send_sem=self.send_sem.at[i],
            recv_sem=self.recv_sem.at[i],
            device_id=device,
            device_id_type=MESH,
        )
        copy.start()
        self.copies.append(copy)
        return copy

    def drain(self):
        for copy in self.copies:
            copy.wait_send()


def gather_line(sender, view, z, x, y, z_peers, x_peer, y_peer, own):
    here = view(z, x, y)
    to_z = [sender.send(own, here, peer) for peer in z_peers]
    over_x, over_y = [sender.send(own, here, x_peer)], []
    if y_peer is not None:
        over_y.append(sender.send(own, here, y_peer))
    for k in (1, 3, 2):
        source = lax.rem(z + 4 - k, 4)
        to_z[k - 1].wait_recv()
        block = view(source, x, y)
        over_x.append(sender.send(block, block, x_peer))
        if y_peer is not None:
            over_y.append(sender.send(block, block, y_peer))
    return over_x, over_y


def gather_all(sender, view, half, z, x, y, z_peers, x_peer, y_peer, own):
    over_x, over_y = gather_line(sender, view, z, x, y, z_peers, x_peer, y_peer, own)
    diagonal = []
    for i, k in enumerate((0, 1, 3, 2)):
        source = lax.rem(z + 4 - k, 4)
        over_x[i].wait_recv()
        block = half(source, 1 - x, y, 0)
        diagonal.append(sender.send(block, block, y_peer))
        over_y[i].wait_recv()
        block = half(source, x, 1 - y, 1)
        diagonal.append(sender.send(block, block, x_peer))
    for copy in diagonal:
        copy.wait_recv()


def gather_kernel(own_ref, all_ref, send_sem, recv_sem, local_sem):
    z, x, y, z_peers, x_peer, y_peer = place()
    width = own_ref.shape[1] // 2
    view = lambda zz, xx, yy: all_ref.at[yy * 8 + zz * 2 + xx]
    half = lambda zz, xx, yy, h: all_ref.at[yy * 8 + zz * 2 + xx, :, pl.ds(h * width, width)]
    greet(z_peers + [x_peer, y_peer])
    local = pltpu.make_async_copy(own_ref, view(z, x, y), local_sem)
    local.start()
    sender = Sender(send_sem, recv_sem)
    gather_all(sender, view, half, z, x, y, z_peers, x_peer, y_peer, own_ref)
    sender.drain()
    local.wait()


def gather_samples(samples):
    rows, width = samples.shape
    gathered = pl.pallas_call(
        gather_kernel,
        out_shape=jax.ShapeDtypeStruct((16, rows, width), samples.dtype),
        in_specs=[pl.BlockSpec(memory_space=pl.ANY)],
        out_specs=pl.BlockSpec(memory_space=pl.ANY),
        scratch_shapes=[
            pltpu.SemaphoreType.DMA((19,)),
            pltpu.SemaphoreType.DMA((19,)),
            pltpu.SemaphoreType.DMA,
        ],
        compiler_params=pltpu.CompilerParams(collective_id=1, has_side_effects=True),
        cost_estimate=pl.CostEstimate(flops=0, bytes_accessed=100_000_000, transcendentals=0),
    )(samples)
    return gathered.reshape(16 * rows, width)


ORDER = (2, 1, 3, 0)
ARRIVAL = (0, 1, 3, 2)
CHUNKS = 2


def interleave(first, second, schedule):
    for which in schedule:
        next((first, second)[which])


def map_steps(
    chunk, sender, spot, cut, part, base, mapped, low, from_y, from_x, to_x, to_y, late_x, late_y, to_z, from_z
):
    z, x, y, z_peers, x_peer, y_peer = spot
    rows, width = base.shape
    span = rows // CHUNKS
    cols = lambda zz, xx: pl.ds(pl.multiple_of((zz * 2 + xx) * width, width), width)
    top_rows = lambda yy: pl.ds(pl.multiple_of(yy * rows + chunk * span, 16), cut)
    low_rows = lambda yy: pl.ds(pl.multiple_of(yy * rows + chunk * span + cut, 16), span - cut)
    lane = lambda xx: pl.ds(pl.multiple_of(xx * width, width), width)
    here = slice(chunk * span, (chunk + 1) * span)
    from_y, from_x, to_x, to_y, late_x, late_y, to_z, from_z = (
        ref.at[chunk] for ref in (from_y, from_x, to_x, to_y, late_x, late_y, to_z, from_z)
    )
    first_y, first_x, second_x, second_y, third = {}, {}, {}, {}, {}
    for k in ORDER:
        zz = lax.rem(z + k, 4)
        pair = pl.ds(pl.multiple_of(zz * 2 * width, 2 * width), 2 * width)
        first_y[k] = sender.send(part.at[top_rows(1 - y), pair], from_y.at[k], y_peer)
        first_x[k] = [
            sender.send(part.at[low_rows(yy), cols(zz, 1 - x)], from_x.at[k, yy], x_peer) for yy in (0, 1)
        ]
        yield
    for k in ORDER:
        zz = lax.rem(z + k, 4)
        first_y[k].wait_recv()
        to_x[k] = (
            part[top_rows(y), cols(zz, 1 - x)].astype(F32) + from_y[k, :, lane(1 - x)].astype(F32)
        ).astype(BF16)
        second_x[k] = sender.send(to_x.at[k], late_x.at[k], x_peer)
        for copy in first_x[k]:
            copy.wait_recv()
        to_y[k] = (
            part[low_rows(1 - y), cols(zz, x)].astype(F32) + from_x[k, 1 - y].astype(F32)
        ).astype(BF16)
        second_y[k] = sender.send(to_y.at[k], late_y.at[k], y_peer)
        yield
    for k in ORDER:
        zz = lax.rem(z + k, 4)
        second_x[k].wait_recv()
        top = (
            part[top_rows(y), cols(zz, x)].astype(F32)
            + from_y[k, :, lane(x)].astype(F32)
            + late_x[k].astype(F32)
        )
        second_y[k].wait_recv()
        bottom = (
            part[low_rows(y), cols(zz, x)].astype(F32) + from_x[k, y].astype(F32) + late_y[k].astype(F32)
        )
        if k:
            to_z[k - 1, :cut] = top.astype(BF16)
            to_z[k - 1, cut:] = bottom.astype(BF16)
            third[k] = sender.send(to_z.at[k - 1], from_z.at[k - 1], z_peers[k - 1])
        else:
            total = jnp.concatenate([top, bottom], axis=0) + base[here].astype(F32)
        yield
    for k in (1, 2, 3):
        third[k].wait_recv()
    total = total + (from_z[0].astype(F32) + from_z[1].astype(F32) + from_z[2].astype(F32))
    mapped[here] = total
    low[here, cols(z, x)] = total.astype(BF16)
    own = low.at[here, cols(z, x)]
    to_line = [sender.send(own, own, peer) for peer in z_peers]
    over_x = [sender.send(own, own, x_peer)]
    yield
    for k in (1, 3, 2):
        to_line[k - 1].wait_recv()
        block = low.at[here, cols(lax.rem(z + 4 - k, 4), x)]
        over_x.append(sender.send(block, block, x_peer))
        yield
    for copy in over_x:
        copy.wait_recv()
    yield


MAP_SCHEDULE = [0] * 4 + [0, 1] * 8 + [0, 1, 1, 0, 1, 0, 1, 0, 1, 1, 1, 1, 1, 0]


def map_kernel(part, base, mapped, low, *rest):
    scratch, (send_sem, recv_sem) = rest[:-2], rest[-2:]
    spot = place()
    greet(spot[3] + list(spot[4:]))
    sender = Sender(send_sem, recv_sem)
    cut = scratch[2].shape[2]
    steps = [map_steps(c, sender, spot, cut, part, base, mapped, low, *scratch) for c in range(CHUNKS)]
    interleave(steps[0], steps[1], MAP_SCHEDULE)
    sender.drain()


def reduce_map(part, base):
    rows, width = base.shape
    span = rows // CHUNKS
    cut = span // 3 * 2
    return pl.pallas_call(
        map_kernel,
        out_shape=(
            jax.ShapeDtypeStruct((rows, width), F32),
            jax.ShapeDtypeStruct((rows, part.shape[1]), BF16),
        ),
        in_specs=[pl.BlockSpec(memory_space=pltpu.VMEM)] * 2,
        out_specs=[pl.BlockSpec(memory_space=pltpu.VMEM)] * 2,
        scratch_shapes=[
            pltpu.VMEM((CHUNKS, 4, cut, 2 * width), BF16),
            pltpu.VMEM((CHUNKS, 4, 2, span - cut, width), BF16),
            pltpu.VMEM((CHUNKS, 4, cut, width), BF16),
            pltpu.VMEM((CHUNKS, 4, span - cut, width), BF16),
            pltpu.VMEM((CHUNKS, 4, cut, width), BF16),
            pltpu.VMEM((CHUNKS, 4, span - cut, width), BF16),
            pltpu.VMEM((CHUNKS, 3, span, width), BF16),
            pltpu.VMEM((CHUNKS, 3, span, width), BF16),
            pltpu.SemaphoreType.DMA((30 * CHUNKS,)),
            pltpu.SemaphoreType.DMA((30 * CHUNKS,)),
        ],
        compiler_params=pltpu.CompilerParams(collective_id=2, has_side_effects=True),
    )(part, base)


def dual_steps(chunk, sender, spot, part, base, mapped, full, from_x, to_z, from_z):
    z, x, y, z_peers, x_peer, y_peer = spot
    rows, width = base.shape
    span = rows // CHUNKS
    cut = span // 3 * 2
    cols = lambda zz, xx: pl.ds(pl.multiple_of((zz * 2 + xx) * width, width), width)
    here = slice(chunk * span, (chunk + 1) * span)
    view = lambda zz, xx, yy: full.at[
        pl.ds(pl.multiple_of(yy * rows + chunk * span, 16), span), cols(zz, xx)
    ]
    top = lambda zz, xx, yy: full.at[pl.ds(pl.multiple_of(yy * rows + chunk * span, 16), cut), cols(zz, xx)]
    bottom = lambda zz, xx, yy: full.at[
        pl.ds(pl.multiple_of(yy * rows + chunk * span + cut, 16), span - cut), cols(zz, xx)
    ]
    from_x, to_z, from_z = (ref.at[chunk] for ref in (from_x, to_z, from_z))
    first, third = {}, {}
    for k in ORDER:
        first[k] = sender.send(part.at[here, cols(lax.rem(z + k, 4), 1 - x)], from_x.at[k], x_peer)
        yield
    for k in ORDER:
        first[k].wait_recv()
        total = part[here, cols(lax.rem(z + k, 4), x)].astype(F32) + from_x[k].astype(F32)
        if k:
            to_z[k - 1] = total.astype(BF16)
            third[k] = sender.send(to_z.at[k - 1], from_z.at[k - 1], z_peers[k - 1])
        yield
    for k in (1, 2, 3):
        third[k].wait_recv()
    grad = (mapped[here] + total) + (
        from_z[0].astype(F32) + from_z[1].astype(F32) + from_z[2].astype(F32)
    )
    full[pl.ds(pl.multiple_of(y * rows + chunk * span, 16), span), cols(z, x)] = (
        base[here].astype(F32) - grad
    ).astype(BF16)
    own = view(z, x, y)
    to_line = [sender.send(own, own, peer) for peer in z_peers]
    over_x, over_y = [sender.send(own, own, x_peer)], [sender.send(own, own, y_peer)]
    yield
    for k in ARRIVAL[1:]:
        to_line[k - 1].wait_recv()
        block = view(lax.rem(z + 4 - k, 4), x, y)
        over_x.append(sender.send(block, block, x_peer))
        over_y.append(sender.send(block, block, y_peer))
        yield
    diagonal = []
    for i, k in enumerate(ARRIVAL):
        source = lax.rem(z + 4 - k, 4)
        over_x[i].wait_recv()
        block = top(source, 1 - x, y)
        diagonal.append(sender.send(block, block, y_peer))
        over_y[i].wait_recv()
        block = bottom(source, x, 1 - y)
        diagonal.append(sender.send(block, block, x_peer))
        yield
    for copy in diagonal:
        copy.wait_recv()
    yield


DUAL_SCHEDULE = [0] * 4 + [0, 1] * 4 + [0, 1, 0, 1, 0, 1, 0, 1, 1] + [0, 1] * 3 + [0] + [1] * 4 + [0, 1]


def dual_kernel(part, base, mapped, full, from_x, to_z, from_z, send_sem, recv_sem):
    spot = place()
    greet(spot[3] + list(spot[4:]))
    sender = Sender(send_sem, recv_sem)
    steps = [
        dual_steps(c, sender, spot, part, base, mapped, full, from_x, to_z, from_z) for c in range(CHUNKS)
    ]
    interleave(steps[0], steps[1], DUAL_SCHEDULE)
    sender.drain()


def reduce_dual(part, base, mapped):
    rows, width = base.shape
    span = rows // CHUNKS
    return pl.pallas_call(
        dual_kernel,
        out_shape=jax.ShapeDtypeStruct((2 * rows, part.shape[1]), BF16),
        in_specs=[pl.BlockSpec(memory_space=pltpu.VMEM)] * 3,
        out_specs=pl.BlockSpec(memory_space=pltpu.VMEM),
        scratch_shapes=[
            pltpu.VMEM((CHUNKS, 4, span, width), BF16),
            pltpu.VMEM((CHUNKS, 3, span, width), BF16),
            pltpu.VMEM((CHUNKS, 3, span, width), BF16),
            pltpu.SemaphoreType.DMA((26 * CHUNKS,)),
            pltpu.SemaphoreType.DMA((26 * CHUNKS,)),
        ],
        compiler_params=pltpu.CompilerParams(collective_id=3, has_side_effects=True),
    )(part, base, mapped)


def chip_body(
    samples,
    dual_weight,
    dual_vector,
    map_weight,
    map_vector,
    moment_weight,
    square_weight,
    moment_vector,
    square_vector,
):
    swap = [(0, 1), (1, 0), (2, 3), (3, 2)]
    fsdp, rep = lax.axis_index("fsdp"), lax.axis_index("rep")
    weight = map_weight.astype(BF16)
    vector = map_vector.astype(BF16)
    weights = (weight, lax.ppermute(weight, "rep", swap))
    vectors = (vector, lax.ppermute(vector, "rep", swap))
    rows = gather_samples(samples)
    inverse_rows = 1.0 / (rows.shape[0] * 2)
    sigmas, scales = [], []
    for block, pair in zip(weights, vectors):
        sigma = jax.nn.sigmoid(contract_last(rows, block) + pair[1].astype(F32))
        sigmas.append(sigma)
        scales.append((pair[0].astype(F32) * sigma).astype(BF16))
    part = (
        jnp.dot(scales[0], weights[0], preferred_element_type=F32)
        + jnp.dot(scales[1], weights[1], preferred_element_type=F32)
    ).astype(BF16)
    half, width = rows.shape[0] // 2, rows.shape[1] // 8
    base = lax.dynamic_slice(rows, ((rep // 2) * half, fsdp * width), (half, width))
    mapped, mapped_low = reduce_map(part, base)
    dual_hidden = contract_last(mapped_low, dual_weight) + dual_vector[1]
    dual_scaled = (dual_vector[0] * jax.nn.sigmoid(dual_hidden)).astype(BF16)
    dual_part = jnp.dot(dual_scaled, dual_weight, preferred_element_type=F32).astype(BF16)
    residual = reduce_dual(dual_part, base, mapped)
    grads, smalls = [], []
    for block, pair, sigma, scaled in zip(weights[::-1], vectors[::-1], sigmas[::-1], scales[::-1]):
        readout = pair[0].astype(F32)
        pulled = contract_last(residual, block)
        curve = readout * (sigma * (1.0 - sigma)) * pulled
        grads.append(contract_first(scaled, residual) + contract_first(curve.astype(BF16), rows))
        smalls.append(jnp.stack([jnp.sum(sigma * pulled, axis=0), jnp.sum(curve, axis=0)]))
    owner_weight = (grads[1] + lax.ppermute(grads[0], "rep", swap)) * inverse_rows
    owner_vector = (smalls[1] + lax.ppermute(smalls[0], "rep", swap)) * inverse_rows
    next_weight, next_moment_weight, next_square_weight = adam_update(
        map_weight, owner_weight, moment_weight, square_weight
    )
    raw_vector, next_moment_vector, next_square_vector = adam_update(
        map_vector, owner_vector, moment_vector, square_vector
    )
    next_vector = jnp.concatenate([jnp.maximum(raw_vector[0:1], 0.0), raw_vector[1:2]], axis=0)
    return (
        next_weight,
        next_vector,
        next_moment_weight,
        next_square_weight,
        next_moment_vector,
        next_square_vector,
    )


def body(
    samples,
    dual_weight,
    dual_vector,
    map_weight,
    map_vector,
    moment_weight,
    square_weight,
    moment_vector,
    square_vector,
):
    group_rows = lax.all_gather(samples, "fsdp", axis=0, tiled=True)
    weight_slab, vector_slab = (
        lax.all_gather(map_weight.astype(jnp.bfloat16), "rep", axis=0, tiled=True),
        lax.all_gather(map_vector.astype(jnp.bfloat16), "rep", axis=1, tiled=True),
    )
    readout = vector_slab[0].astype(jnp.float32)
    offset = vector_slab[1].astype(jnp.float32)
    inverse_rows = 1.0 / (group_rows.shape[0] * lax.axis_size("rep"))
    hidden = contract_last(group_rows, weight_slab) + offset
    sigma = jax.nn.sigmoid(hidden)
    scaled = (readout * sigma).astype(jnp.bfloat16)
    group_float = group_rows.astype(jnp.float32)
    mapped = group_float + lax.psum(
        jnp.dot(scaled, weight_slab, preferred_element_type=jnp.float32).astype(jnp.bfloat16),
        "fsdp",
    ).astype(jnp.float32)
    mapped_low = mapped.astype(jnp.bfloat16)
    dual_hidden = contract_last(mapped_low, dual_weight) + dual_vector[1]
    dual_scaled = (dual_vector[0] * jax.nn.sigmoid(dual_hidden)).astype(jnp.bfloat16)
    dual_grad = mapped + lax.psum(
        jnp.dot(dual_scaled, dual_weight, preferred_element_type=jnp.float32).astype(jnp.bfloat16),
        "fsdp",
    ).astype(jnp.float32)
    residual = (group_float - dual_grad).astype(jnp.bfloat16)
    pulled = contract_last(residual, weight_slab)
    slope = sigma * (1.0 - sigma)
    curve_float = readout * slope * pulled
    curve_term = curve_float.astype(jnp.bfloat16)
    left_stack = jnp.concatenate([scaled, curve_term], axis=0)
    right_stack = jnp.concatenate([residual, group_rows], axis=0)
    grad_slab = contract_first(left_stack, right_stack) * inverse_rows
    grad_small = (
        jnp.stack([jnp.sum(sigma * pulled, axis=0), jnp.sum(curve_float, axis=0)]) * inverse_rows
    )
    owner_weight, owner_vector = (
        lax.psum_scatter(grad_slab, "rep", scatter_dimension=0, tiled=True),
        lax.psum_scatter(grad_small, "rep", scatter_dimension=1, tiled=True),
    )
    next_weight, next_moment_weight, next_square_weight = adam_update(
        map_weight, owner_weight, moment_weight, square_weight
    )
    raw_vector, next_moment_vector, next_square_vector = adam_update(
        map_vector, owner_vector, moment_vector, square_vector
    )
    next_vector = jnp.concatenate([jnp.maximum(raw_vector[0:1], 0.0), raw_vector[1:2]], axis=0)
    return (
        next_weight,
        next_vector,
        next_moment_weight,
        next_square_weight,
        next_moment_vector,
        next_square_vector,
    )


def solution(mesh):
    by_chip = mesh.shape["fsdp"] == 8 and mesh.shape["rep"] == 4
    return jax.shard_map(
        chip_body if by_chip else body,
        mesh=mesh,
        in_specs=(
            P(("fsdp", "rep"), None),
            P("fsdp", None),
            P(None, "fsdp"),
            P(("fsdp", "rep"), None),
            P(None, ("fsdp", "rep")),
            P(("fsdp", "rep"), None),
            P(("fsdp", "rep"), None),
            P(None, ("fsdp", "rep")),
            P(None, ("fsdp", "rep")),
        ),
        out_specs=(
            P(("fsdp", "rep"), None),
            P(None, ("fsdp", "rep")),
            P(("fsdp", "rep"), None),
            P(("fsdp", "rep"), None),
            P(None, ("fsdp", "rep")),
            P(None, ("fsdp", "rep")),
        ),
        check_vma=False,
    )
```

```python
import jax
import jax.numpy as jnp
from jax import lax
from jax.experimental import pallas as pl
from jax.experimental.pallas import tpu as pltpu
from jax.sharding import PartitionSpec as P

beta_one = 0.9
beta_two = 0.999
learn_rate = 0.001
epsilon = 1e-08
adam_step = 10


def contract_last(left, right):
    return lax.dot_general(
        left, right, (((1,), (1,)), ((), ())), preferred_element_type=jnp.float32
    )


def contract_first(left, right):
    return lax.dot_general(
        left, right, (((0,), (0,)), ((), ())), preferred_element_type=jnp.float32
    )


def adam_update(param, grad, moment, square):
    moment_new = beta_one * moment + (1.0 - beta_one) * grad
    square_new = beta_two * square + (1.0 - beta_two) * grad * grad
    fix_one = 1.0 - beta_one**adam_step
    fix_two = 1.0 - beta_two**adam_step
    update = learn_rate * (moment_new / fix_one) / (jnp.sqrt(square_new / fix_two) + epsilon)
    return (param - update, moment_new, square_new)


MESH = pl.DeviceIdType.MESH
F32 = jnp.float32
BF16 = jnp.bfloat16


def place():
    fsdp, rep = lax.axis_index("fsdp"), lax.axis_index("rep")
    z, x = fsdp // 2, fsdp % 2
    y, core = rep // 2, rep % 2
    z_peers = [(lax.rem(z + k, 4) * 2 + x, rep) for k in (1, 2, 3)]
    x_peer = (z * 2 + 1 - x, rep)
    y_peer = (fsdp, (1 - y) * 2 + core)
    return z, x, y, z_peers, x_peer, y_peer


def greet(peers):
    barrier = pltpu.get_barrier_semaphore()
    for peer in peers:
        pl.semaphore_signal(barrier, inc=1, device_id=peer, device_id_type=MESH)
    pl.semaphore_wait(barrier, len(peers))


class Sender:
    def __init__(self, send_sem, recv_sem):
        self.send_sem, self.recv_sem, self.copies = send_sem, recv_sem, []

    def send(self, src, dst, device):
        i = len(self.copies)
        copy = pltpu.make_async_remote_copy(
            src_ref=src,
            dst_ref=dst,
            send_sem=self.send_sem.at[i],
            recv_sem=self.recv_sem.at[i],
            device_id=device,
            device_id_type=MESH,
        )
        copy.start()
        self.copies.append(copy)
        return copy

    def drain(self):
        for copy in self.copies:
            copy.wait_send()


def gather_steps(sender, view, top, bottom, spot, source_ref=None):
    z, x, y, z_peers, x_peer, y_peer = spot
    place_own = view(z, x, y)
    own = place_own if source_ref is None else source_ref
    to_line = [sender.send(own, place_own, z_peers[k - 1]) for k in (1, 2, 3)]
    over_x, over_y = [sender.send(own, place_own, x_peer)], [sender.send(own, place_own, y_peer)]
    diagonal = []
    yield

    def cross(i):
        source = lax.rem(z + 4 - ARRIVAL[i], 4)
        over_x[i].wait_recv()
        block = top(source, 1 - x, y)
        diagonal.append(sender.send(block, block, y_peer))
        over_y[i].wait_recv()
        block = bottom(source, x, 1 - y)
        diagonal.append(sender.send(block, block, x_peer))

    for i, k in enumerate(ARRIVAL):
        if i:
            to_line[k - 1].wait_recv()
            block = view(lax.rem(z + 4 - k, 4), x, y)
            over_x.append(sender.send(block, block, x_peer))
            over_y.append(sender.send(block, block, y_peer))
            yield
            cross(i - 1)
            yield
    cross(3)
    yield
    for copy in diagonal:
        copy.wait_recv()
    yield


def gather_kernel(own_ref, weight_ref, all_ref, weight_own, weight_other, wide, send_sem, recv_sem, local_sem):
    spot = place()
    z, x, y, z_peers, x_peer, y_peer = spot
    width = own_ref.shape[1] // 2
    view = lambda zz, xx, yy: all_ref.at[yy * 8 + zz * 2 + xx]
    top = lambda zz, xx, yy: all_ref.at[yy * 8 + zz * 2 + xx, :, pl.ds(0, width)]
    bottom = lambda zz, xx, yy: all_ref.at[yy * 8 + zz * 2 + xx, :, pl.ds(width, width)]
    fsdp, rep = x_peer[0] + 2 * x - 1, x_peer[1]
    partner = (fsdp, rep + 1 - 2 * lax.rem(rep, 2))
    local = pltpu.make_async_copy(own_ref, view(z, x, y), local_sem.at[0])
    local.start()
    load = pltpu.make_async_copy(weight_ref, wide, local_sem.at[1])
    load.start()
    greet(z_peers + [x_peer, y_peer, partner])
    sender = Sender(send_sem, recv_sem)
    steps = gather_steps(sender, view, top, bottom, spot, own_ref)
    next(steps)
    load.wait()
    weight_own[...] = wide[...].astype(BF16)
    swapped = sender.send(weight_own, weight_other, partner)
    for _ in steps:
        pass
    swapped.wait_recv()
    local.wait()
    sender.drain()


def gather_samples(samples, weight):
    rows, width = samples.shape
    low = jax.ShapeDtypeStruct(weight.shape, BF16)
    gathered, own, other = pl.pallas_call(
        gather_kernel,
        out_shape=(jax.ShapeDtypeStruct((16, rows, width), samples.dtype), low, low),
        in_specs=[pl.BlockSpec(memory_space=pl.ANY)] * 2,
        out_specs=[
            pl.BlockSpec(memory_space=pl.ANY),
            pl.BlockSpec(memory_space=pltpu.VMEM),
            pl.BlockSpec(memory_space=pltpu.VMEM),
        ],
        scratch_shapes=[
            pltpu.VMEM(weight.shape, F32),
            pltpu.SemaphoreType.DMA((20,)),
            pltpu.SemaphoreType.DMA((20,)),
            pltpu.SemaphoreType.DMA((2,)),
        ],
        compiler_params=pltpu.CompilerParams(collective_id=1, has_side_effects=True),
        cost_estimate=pl.CostEstimate(flops=0, bytes_accessed=100_000_000, transcendentals=0),
    )(samples, weight)
    return gathered.reshape(16 * rows, width), (own, other)


ORDER = (2, 1, 3, 0)
ARRIVAL = (0, 1, 3, 2)
CHUNKS = 2


def interleave(first, second, schedule):
    for which in schedule:
        next((first, second)[which])


def map_steps(
    chunk, sender, spot, cut, fill, part, base, mapped, low, from_y, from_x, to_x, to_y, late_x, late_y, to_z, from_z
):
    z, x, y, z_peers, x_peer, y_peer = spot
    rows, width = base.shape
    span = rows // CHUNKS
    cols = lambda zz, xx: pl.ds(pl.multiple_of((zz * 2 + xx) * width, width), width)
    top_rows = lambda yy: pl.ds(pl.multiple_of(yy * rows + chunk * span, 16), cut)
    low_rows = lambda yy: pl.ds(pl.multiple_of(yy * rows + chunk * span + cut, 16), span - cut)
    lane = lambda xx: pl.ds(pl.multiple_of(xx * width, width), width)
    here = slice(chunk * span, (chunk + 1) * span)
    from_y, from_x, to_x, to_y, late_x, late_y, to_z, from_z = (
        ref.at[chunk] for ref in (from_y, from_x, to_x, to_y, late_x, late_y, to_z, from_z)
    )
    first_y, first_x, second_x, second_y, third = {}, {}, {}, {}, {}
    for k in ORDER:
        zz = lax.rem(z + k, 4)
        pair = pl.ds(pl.multiple_of(zz * 2 * width, 2 * width), 2 * width)
        if chunk == 0:
            fill(k, pair)
        first_y[k] = sender.send(part.at[top_rows(1 - y), pair], from_y.at[k], y_peer)
        first_x[k] = [
            sender.send(part.at[low_rows(yy), cols(zz, 1 - x)], from_x.at[k, yy], x_peer) for yy in (0, 1)
        ]
        yield
    for k in ORDER:
        zz = lax.rem(z + k, 4)
        first_y[k].wait_recv()
        to_x[k] = (
            part[top_rows(y), cols(zz, 1 - x)].astype(F32) + from_y[k, :, lane(1 - x)].astype(F32)
        ).astype(BF16)
        second_x[k] = sender.send(to_x.at[k], late_x.at[k], x_peer)
        for copy in first_x[k]:
            copy.wait_recv()
        to_y[k] = (
            part[low_rows(1 - y), cols(zz, x)].astype(F32) + from_x[k, 1 - y].astype(F32)
        ).astype(BF16)
        second_y[k] = sender.send(to_y.at[k], late_y.at[k], y_peer)
        yield
    for k in ORDER:
        zz = lax.rem(z + k, 4)
        second_x[k].wait_recv()
        top = (
            part[top_rows(y), cols(zz, x)].astype(F32)
            + from_y[k, :, lane(x)].astype(F32)
            + late_x[k].astype(F32)
        )
        second_y[k].wait_recv()
        bottom = (
            part[low_rows(y), cols(zz, x)].astype(F32) + from_x[k, y].astype(F32) + late_y[k].astype(F32)
        )
        if k:
            to_z[k - 1, :cut] = top.astype(BF16)
            to_z[k - 1, cut:] = bottom.astype(BF16)
            third[k] = sender.send(to_z.at[k - 1], from_z.at[k - 1], z_peers[k - 1])
        else:
            total = jnp.concatenate([top, bottom], axis=0) + base[here].astype(F32)
        yield
    for k in (1, 2, 3):
        third[k].wait_recv()
    total = total + (from_z[0].astype(F32) + from_z[1].astype(F32) + from_z[2].astype(F32))
    mapped[here] = total
    low[here, cols(z, x)] = total.astype(BF16)
    own = low.at[here, cols(z, x)]
    to_line = [sender.send(own, own, peer) for peer in z_peers]
    over_x = [sender.send(own, own, x_peer)]
    yield
    for k in (1, 3, 2):
        to_line[k - 1].wait_recv()
        block = low.at[here, cols(lax.rem(z + 4 - k, 4), x)]
        over_x.append(sender.send(block, block, x_peer))
        yield
    for copy in over_x:
        copy.wait_recv()
    yield


MAP_SCHEDULE = [0] * 4 + [0, 1] * 8 + [0, 1, 1, 0, 1, 0, 1, 0, 1, 1, 1, 1, 1, 0]


def stream_columns(z, pairs, local_sem, width):
    loads = {}
    for k in ORDER:
        span = pl.ds(pl.multiple_of(lax.rem(z + k, 4) * width, width), width)
        loads[k] = [
            pltpu.make_async_copy(source.at[:, span], held.at[k], local_sem.at[i, k])
            for i, (source, held) in enumerate(pairs)
        ]
        for load in loads[k]:
            load.start()
    return loads


def map_kernel(left_own, left_other, weight_own, weight_other, base, mapped, low, *rest):
    part, held_own, held_other = rest[:3]
    scratch, (send_sem, recv_sem, local_sem) = rest[3:-3], rest[-3:]
    spot = place()
    loads = stream_columns(
        spot[0], ((weight_own, held_own), (weight_other, held_other)), local_sem, held_own.shape[2]
    )

    def fill(k, pair):
        for load in loads[k]:
            load.wait()
        part[:, pair] = (
            jnp.dot(left_own[...], held_own[k], preferred_element_type=F32)
            + jnp.dot(left_other[...], held_other[k], preferred_element_type=F32)
        ).astype(BF16)

    greet(spot[3] + list(spot[4:]))
    sender = Sender(send_sem, recv_sem)
    cut = scratch[2].shape[2]
    steps = [map_steps(c, sender, spot, cut, fill, part, base, mapped, low, *scratch) for c in range(CHUNKS)]
    interleave(steps[0], steps[1], MAP_SCHEDULE)
    sender.drain()


def reduce_map(lefts, weights, base):
    rows, width = base.shape
    span = rows // CHUNKS
    cut = span // 3 * 2
    return pl.pallas_call(
        map_kernel,
        out_shape=(
            jax.ShapeDtypeStruct((rows, width), F32),
            jax.ShapeDtypeStruct((rows, 8 * width), BF16),
        ),
        in_specs=[
            pl.BlockSpec(memory_space=pltpu.VMEM),
            pl.BlockSpec(memory_space=pltpu.VMEM),
            pl.BlockSpec(memory_space=pl.ANY),
            pl.BlockSpec(memory_space=pl.ANY),
            pl.BlockSpec(memory_space=pltpu.VMEM),
        ],
        out_specs=[pl.BlockSpec(memory_space=pltpu.VMEM)] * 2,
        scratch_shapes=[
            pltpu.VMEM((2 * rows, 8 * width), BF16),
            pltpu.VMEM((4, weights[0].shape[0], 2 * width), BF16),
            pltpu.VMEM((4, weights[1].shape[0], 2 * width), BF16),
            pltpu.VMEM((CHUNKS, 4, cut, 2 * width), BF16),
            pltpu.VMEM((CHUNKS, 4, 2, span - cut, width), BF16),
            pltpu.VMEM((CHUNKS, 4, cut, width), BF16),
            pltpu.VMEM((CHUNKS, 4, span - cut, width), BF16),
            pltpu.VMEM((CHUNKS, 4, cut, width), BF16),
            pltpu.VMEM((CHUNKS, 4, span - cut, width), BF16),
            pltpu.VMEM((CHUNKS, 3, span, width), BF16),
            pltpu.VMEM((CHUNKS, 3, span, width), BF16),
            pltpu.SemaphoreType.DMA((30 * CHUNKS,)),
            pltpu.SemaphoreType.DMA((30 * CHUNKS,)),
            pltpu.SemaphoreType.DMA((2, 4)),
        ],
        compiler_params=pltpu.CompilerParams(collective_id=2, has_side_effects=True),
    )(*lefts, *weights, base)


def dual_steps(chunk, sender, spot, fill, part, base, mapped, full, from_x, to_z, from_z):
    z, x, y, z_peers, x_peer, y_peer = spot
    rows, width = base.shape
    span = rows // CHUNKS
    cut = span // 3 * 2
    cols = lambda zz, xx: pl.ds(pl.multiple_of((zz * 2 + xx) * width, width), width)
    here = slice(chunk * span, (chunk + 1) * span)
    view = lambda zz, xx, yy: full.at[
        pl.ds(pl.multiple_of(yy * rows + chunk * span, 16), span), cols(zz, xx)
    ]
    top = lambda zz, xx, yy: full.at[pl.ds(pl.multiple_of(yy * rows + chunk * span, 16), cut), cols(zz, xx)]
    bottom = lambda zz, xx, yy: full.at[
        pl.ds(pl.multiple_of(yy * rows + chunk * span + cut, 16), span - cut), cols(zz, xx)
    ]
    from_x, to_z, from_z = (ref.at[chunk] for ref in (from_x, to_z, from_z))
    first, third = {}, {}
    for k in ORDER:
        if chunk == 0:
            fill(k, pl.ds(pl.multiple_of(lax.rem(z + k, 4) * 2 * width, 2 * width), 2 * width))
        first[k] = sender.send(part.at[here, cols(lax.rem(z + k, 4), 1 - x)], from_x.at[k], x_peer)
        yield
    for k in ORDER:
        first[k].wait_recv()
        total = part[here, cols(lax.rem(z + k, 4), x)].astype(F32) + from_x[k].astype(F32)
        if k:
            to_z[k - 1] = total.astype(BF16)
            third[k] = sender.send(to_z.at[k - 1], from_z.at[k - 1], z_peers[k - 1])
        yield
    for k in (1, 2, 3):
        third[k].wait_recv()
    grad = (mapped[here] + total) + (
        from_z[0].astype(F32) + from_z[1].astype(F32) + from_z[2].astype(F32)
    )
    full[pl.ds(pl.multiple_of(y * rows + chunk * span, 16), span), cols(z, x)] = (
        base[here].astype(F32) - grad
    ).astype(BF16)
    yield from gather_steps(sender, view, top, bottom, spot)


DUAL_SCHEDULE = [0] * 4 + [0, 1] * 4 + [0, 1, 0, 1, 0, 1, 0, 1, 1] + [0, 1] * 3 + [0] + [1] * 4 + [0, 1]


def dual_kernel(left, weight, base, mapped, full, part, held, from_x, to_z, from_z, send_sem, recv_sem, local_sem):
    spot = place()
    loads = stream_columns(spot[0], ((weight, held),), local_sem, held.shape[2])

    def fill(k, pair):
        loads[k][0].wait()
        part[:, pair] = jnp.dot(left[...], held[k], preferred_element_type=F32).astype(BF16)

    greet(spot[3] + list(spot[4:]))
    sender = Sender(send_sem, recv_sem)
    steps = [
        dual_steps(c, sender, spot, fill, part, base, mapped, full, from_x, to_z, from_z) for c in range(CHUNKS)
    ]
    interleave(steps[0], steps[1], DUAL_SCHEDULE)
    sender.drain()


def reduce_dual(left, weight, base, mapped):
    rows, width = base.shape
    span = rows // CHUNKS
    return pl.pallas_call(
        dual_kernel,
        out_shape=jax.ShapeDtypeStruct((2 * rows, weight.shape[1]), BF16),
        in_specs=[
            pl.BlockSpec(memory_space=pltpu.VMEM),
            pl.BlockSpec(memory_space=pl.ANY),
            pl.BlockSpec(memory_space=pltpu.VMEM),
            pl.BlockSpec(memory_space=pltpu.VMEM),
        ],
        out_specs=pl.BlockSpec(memory_space=pltpu.VMEM),
        scratch_shapes=[
            pltpu.VMEM((rows, 8 * width), BF16),
            pltpu.VMEM((4, weight.shape[0], 2 * width), BF16),
            pltpu.VMEM((CHUNKS, 4, span, width), BF16),
            pltpu.VMEM((CHUNKS, 3, span, width), BF16),
            pltpu.VMEM((CHUNKS, 3, span, width), BF16),
            pltpu.SemaphoreType.DMA((26 * CHUNKS,)),
            pltpu.SemaphoreType.DMA((26 * CHUNKS,)),
            pltpu.SemaphoreType.DMA((1, 4)),
        ],
        compiler_params=pltpu.CompilerParams(collective_id=3, has_side_effects=True),
    )(left, weight, base, mapped)


def chip_body(
    samples,
    dual_weight,
    dual_vector,
    map_weight,
    map_vector,
    moment_weight,
    square_weight,
    moment_vector,
    square_vector,
):
    swap = [(0, 1), (1, 0), (2, 3), (3, 2)]
    fsdp, rep = lax.axis_index("fsdp"), lax.axis_index("rep")
    vector = map_vector.astype(BF16)
    vectors = (vector, lax.ppermute(vector, "rep", swap))
    rows, weights = gather_samples(samples, map_weight)
    inverse_rows = 1.0 / (rows.shape[0] * 2)
    sigmas, scales = [], []
    for block, pair in zip(weights, vectors):
        sigma = jax.nn.sigmoid(contract_last(rows, block) + pair[1].astype(F32))
        sigmas.append(sigma)
        scales.append((pair[0].astype(F32) * sigma).astype(BF16))
    half, width = rows.shape[0] // 2, rows.shape[1] // 8
    base = lax.dynamic_slice(rows, ((rep // 2) * half, fsdp * width), (half, width))
    mapped, mapped_low = reduce_map(scales, weights, base)
    dual_hidden = contract_last(mapped_low, dual_weight) + dual_vector[1]
    dual_scaled = (dual_vector[0] * jax.nn.sigmoid(dual_hidden)).astype(BF16)
    residual = reduce_dual(dual_scaled, dual_weight, base, mapped)
    grads, smalls = [], []
    for block, pair, sigma, scaled in zip(weights[::-1], vectors[::-1], sigmas[::-1], scales[::-1]):
        readout = pair[0].astype(F32)
        pulled = contract_last(residual, block)
        curve = readout * (sigma * (1.0 - sigma)) * pulled
        grads.append(contract_first(scaled, residual) + contract_first(curve.astype(BF16), rows))
        smalls.append(jnp.stack([jnp.sum(sigma * pulled, axis=0), jnp.sum(curve, axis=0)]))
    owner_weight = (grads[1] + lax.ppermute(grads[0], "rep", swap)) * inverse_rows
    owner_vector = (smalls[1] + lax.ppermute(smalls[0], "rep", swap)) * inverse_rows
    next_weight, next_moment_weight, next_square_weight = adam_update(
        map_weight, owner_weight, moment_weight, square_weight
    )
    raw_vector, next_moment_vector, next_square_vector = adam_update(
        map_vector, owner_vector, moment_vector, square_vector
    )
    next_vector = jnp.concatenate([jnp.maximum(raw_vector[0:1], 0.0), raw_vector[1:2]], axis=0)
    return (
        next_weight,
        next_vector,
        next_moment_weight,
        next_square_weight,
        next_moment_vector,
        next_square_vector,
    )


def body(
    samples,
    dual_weight,
    dual_vector,
    map_weight,
    map_vector,
    moment_weight,
    square_weight,
    moment_vector,
    square_vector,
):
    group_rows = lax.all_gather(samples, "fsdp", axis=0, tiled=True)
    weight_slab, vector_slab = (
        lax.all_gather(map_weight.astype(jnp.bfloat16), "rep", axis=0, tiled=True),
        lax.all_gather(map_vector.astype(jnp.bfloat16), "rep", axis=1, tiled=True),
    )
    readout = vector_slab[0].astype(jnp.float32)
    offset = vector_slab[1].astype(jnp.float32)
    inverse_rows = 1.0 / (group_rows.shape[0] * lax.axis_size("rep"))
    hidden = contract_last(group_rows, weight_slab) + offset
    sigma = jax.nn.sigmoid(hidden)
    scaled = (readout * sigma).astype(jnp.bfloat16)
    group_float = group_rows.astype(jnp.float32)
    mapped = group_float + lax.psum(
        jnp.dot(scaled, weight_slab, preferred_element_type=jnp.float32).astype(jnp.bfloat16),
        "fsdp",
    ).astype(jnp.float32)
    mapped_low = mapped.astype(jnp.bfloat16)
    dual_hidden = contract_last(mapped_low, dual_weight) + dual_vector[1]
    dual_scaled = (dual_vector[0] * jax.nn.sigmoid(dual_hidden)).astype(jnp.bfloat16)
    dual_grad = mapped + lax.psum(
        jnp.dot(dual_scaled, dual_weight, preferred_element_type=jnp.float32).astype(jnp.bfloat16),
        "fsdp",
    ).astype(jnp.float32)
    residual = (group_float - dual_grad).astype(jnp.bfloat16)
    pulled = contract_last(residual, weight_slab)
    slope = sigma * (1.0 - sigma)
    curve_float = readout * slope * pulled
    curve_term = curve_float.astype(jnp.bfloat16)
    left_stack = jnp.concatenate([scaled, curve_term], axis=0)
    right_stack = jnp.concatenate([residual, group_rows], axis=0)
    grad_slab = contract_first(left_stack, right_stack) * inverse_rows
    grad_small = (
        jnp.stack([jnp.sum(sigma * pulled, axis=0), jnp.sum(curve_float, axis=0)]) * inverse_rows
    )
    owner_weight, owner_vector = (
        lax.psum_scatter(grad_slab, "rep", scatter_dimension=0, tiled=True),
        lax.psum_scatter(grad_small, "rep", scatter_dimension=1, tiled=True),
    )
    next_weight, next_moment_weight, next_square_weight = adam_update(
        map_weight, owner_weight, moment_weight, square_weight
    )
    raw_vector, next_moment_vector, next_square_vector = adam_update(
        map_vector, owner_vector, moment_vector, square_vector
    )
    next_vector = jnp.concatenate([jnp.maximum(raw_vector[0:1], 0.0), raw_vector[1:2]], axis=0)
    return (
        next_weight,
        next_vector,
        next_moment_weight,
        next_square_weight,
        next_moment_vector,
        next_square_vector,
    )


def solution(mesh):
    by_chip = mesh.shape["fsdp"] == 8 and mesh.shape["rep"] == 4
    return jax.shard_map(
        chip_body if by_chip else body,
        mesh=mesh,
        in_specs=(
            P(("fsdp", "rep"), None),
            P("fsdp", None),
            P(None, "fsdp"),
            P(("fsdp", "rep"), None),
            P(None, ("fsdp", "rep")),
            P(("fsdp", "rep"), None),
            P(("fsdp", "rep"), None),
            P(None, ("fsdp", "rep")),
            P(None, ("fsdp", "rep")),
        ),
        out_specs=(
            P(("fsdp", "rep"), None),
            P(None, ("fsdp", "rep")),
            P(("fsdp", "rep"), None),
            P(("fsdp", "rep"), None),
            P(None, ("fsdp", "rep")),
            P(None, ("fsdp", "rep")),
        ),
        check_vma=False,
    )
```

```python
import jax
import jax.numpy as jnp
from jax import lax
from jax.experimental import pallas as pl
from jax.experimental.pallas import tpu as pltpu
from jax.sharding import PartitionSpec as P

beta_one = 0.9
beta_two = 0.999
learn_rate = 0.001
epsilon = 1e-08
adam_step = 10


def contract_last(left, right):
    return lax.dot_general(
        left, right, (((1,), (1,)), ((), ())), preferred_element_type=jnp.float32
    )


def contract_first(left, right):
    return lax.dot_general(
        left, right, (((0,), (0,)), ((), ())), preferred_element_type=jnp.float32
    )


def adam_update(param, grad, moment, square):
    moment_new = beta_one * moment + (1.0 - beta_one) * grad
    square_new = beta_two * square + (1.0 - beta_two) * grad * grad
    fix_one = 1.0 - beta_one**adam_step
    fix_two = 1.0 - beta_two**adam_step
    update = learn_rate * (moment_new / fix_one) / (jnp.sqrt(square_new / fix_two) + epsilon)
    return (param - update, moment_new, square_new)


MESH = pl.DeviceIdType.MESH
F32 = jnp.float32
BF16 = jnp.bfloat16


def place():
    fsdp, rep = lax.axis_index("fsdp"), lax.axis_index("rep")
    z, x = fsdp // 2, fsdp % 2
    y, core = rep // 2, rep % 2
    z_peers = [(lax.rem(z + k, 4) * 2 + x, rep) for k in (1, 2, 3)]
    x_peer = (z * 2 + 1 - x, rep)
    y_peer = (fsdp, (1 - y) * 2 + core)
    return z, x, y, z_peers, x_peer, y_peer


def greet(peers):
    barrier = pltpu.get_barrier_semaphore()
    for peer in peers:
        pl.semaphore_signal(barrier, inc=1, device_id=peer, device_id_type=MESH)
    pl.semaphore_wait(barrier, len(peers))


class Sender:
    def __init__(self, send_sem, recv_sem):
        self.send_sem, self.recv_sem, self.copies = send_sem, recv_sem, []

    def send(self, src, dst, device):
        i = len(self.copies)
        copy = pltpu.make_async_remote_copy(
            src_ref=src,
            dst_ref=dst,
            send_sem=self.send_sem.at[i],
            recv_sem=self.recv_sem.at[i],
            device_id=device,
            device_id_type=MESH,
        )
        copy.start()
        self.copies.append(copy)
        return copy

    def drain(self):
        for copy in self.copies:
            copy.wait_send()


def gather_steps(sender, view, top, bottom, spot, source_ref=None):
    z, x, y, z_peers, x_peer, y_peer = spot
    place_own = view(z, x, y)
    own = place_own if source_ref is None else source_ref
    to_line = [sender.send(own, place_own, z_peers[k - 1]) for k in (1, 2, 3)]
    over_x, over_y = [sender.send(own, place_own, x_peer)], [sender.send(own, place_own, y_peer)]
    diagonal = []
    yield

    def cross(i):
        source = lax.rem(z + 4 - ARRIVAL[i], 4)
        over_x[i].wait_recv()
        block = top(source, 1 - x, y)
        diagonal.append(sender.send(block, block, y_peer))
        over_y[i].wait_recv()
        block = bottom(source, x, 1 - y)
        diagonal.append(sender.send(block, block, x_peer))

    for i, k in enumerate(ARRIVAL):
        if i:
            to_line[k - 1].wait_recv()
            block = view(lax.rem(z + 4 - k, 4), x, y)
            over_x.append(sender.send(block, block, x_peer))
            over_y.append(sender.send(block, block, y_peer))
            yield
            cross(i - 1)
            yield
    cross(3)
    yield
    for copy in diagonal:
        copy.wait_recv()
    yield


def gather_kernel(own_ref, weight_ref, all_ref, weight_own, weight_other, wide, send_sem, recv_sem, local_sem):
    spot = place()
    z, x, y, z_peers, x_peer, y_peer = spot
    width = own_ref.shape[1] // 2
    view = lambda zz, xx, yy: all_ref.at[yy * 8 + zz * 2 + xx]
    top = lambda zz, xx, yy: all_ref.at[yy * 8 + zz * 2 + xx, :, pl.ds(0, width)]
    bottom = lambda zz, xx, yy: all_ref.at[yy * 8 + zz * 2 + xx, :, pl.ds(width, width)]
    fsdp, rep = x_peer[0] + 2 * x - 1, x_peer[1]
    partner = (fsdp, rep + 1 - 2 * lax.rem(rep, 2))
    local = pltpu.make_async_copy(own_ref, view(z, x, y), local_sem.at[0])
    local.start()
    load = pltpu.make_async_copy(weight_ref, wide, local_sem.at[1])
    load.start()
    greet(z_peers + [x_peer, y_peer, partner])
    sender = Sender(send_sem, recv_sem)
    steps = gather_steps(sender, view, top, bottom, spot, own_ref)
    next(steps)
    load.wait()
    weight_own[...] = wide[...].astype(BF16)
    swapped = sender.send(weight_own, weight_other, partner)
    for _ in steps:
        pass
    swapped.wait_recv()
    local.wait()
    sender.drain()


def gather_samples(samples, weight):
    rows, width = samples.shape
    low = jax.ShapeDtypeStruct(weight.shape, BF16)
    gathered, own, other = pl.pallas_call(
        gather_kernel,
        out_shape=(jax.ShapeDtypeStruct((16, rows, width), samples.dtype), low, low),
        in_specs=[pl.BlockSpec(memory_space=pl.ANY)] * 2,
        out_specs=[
            pl.BlockSpec(memory_space=pl.ANY),
            pl.BlockSpec(memory_space=pltpu.VMEM),
            pl.BlockSpec(memory_space=pltpu.VMEM),
        ],
        scratch_shapes=[
            pltpu.VMEM(weight.shape, F32),
            pltpu.SemaphoreType.DMA((20,)),
            pltpu.SemaphoreType.DMA((20,)),
            pltpu.SemaphoreType.DMA((2,)),
        ],
        compiler_params=pltpu.CompilerParams(collective_id=1, has_side_effects=True),
        cost_estimate=pl.CostEstimate(flops=0, bytes_accessed=100_000_000, transcendentals=0),
    )(samples, weight)
    return gathered.reshape(16 * rows, width), (own, other)


ORDER = (2, 1, 3, 0)
ARRIVAL = (0, 1, 3, 2)
CHUNKS = 2


def interleave(first, second, schedule):
    for which in schedule:
        next((first, second)[which])


def map_steps(
    chunk, sender, spot, cut, fill, part, base, mapped, low, from_y, from_x, to_x, to_y, late_x, late_y, to_z, from_z
):
    z, x, y, z_peers, x_peer, y_peer = spot
    rows, width = base.shape
    span = rows // CHUNKS
    cols = lambda zz, xx: pl.ds(pl.multiple_of((zz * 2 + xx) * width, width), width)
    top_rows = lambda yy: pl.ds(pl.multiple_of(yy * rows + chunk * span, 16), cut)
    low_rows = lambda yy: pl.ds(pl.multiple_of(yy * rows + chunk * span + cut, 16), span - cut)
    lane = lambda xx: pl.ds(pl.multiple_of(xx * width, width), width)
    here = slice(chunk * span, (chunk + 1) * span)
    from_y, from_x, to_x, to_y, late_x, late_y, to_z, from_z = (
        ref.at[chunk] for ref in (from_y, from_x, to_x, to_y, late_x, late_y, to_z, from_z)
    )
    first_y, first_x, second_x, second_y, third = {}, {}, {}, {}, {}
    for k in ORDER:
        zz = lax.rem(z + k, 4)
        pair = pl.ds(pl.multiple_of(zz * 2 * width, 2 * width), 2 * width)
        if chunk == 0:
            fill(k, pair)
        first_y[k] = sender.send(part.at[top_rows(1 - y), pair], from_y.at[k], y_peer)
        first_x[k] = [
            sender.send(part.at[low_rows(yy), cols(zz, 1 - x)], from_x.at[k, yy], x_peer) for yy in (0, 1)
        ]
        yield
    for k in ORDER:
        zz = lax.rem(z + k, 4)
        first_y[k].wait_recv()
        to_x[k] = (
            part[top_rows(y), cols(zz, 1 - x)].astype(F32) + from_y[k, :, lane(1 - x)].astype(F32)
        ).astype(BF16)
        second_x[k] = sender.send(to_x.at[k], late_x.at[k], x_peer)
        for copy in first_x[k]:
            copy.wait_recv()
        to_y[k] = (
            part[low_rows(1 - y), cols(zz, x)].astype(F32) + from_x[k, 1 - y].astype(F32)
        ).astype(BF16)
        second_y[k] = sender.send(to_y.at[k], late_y.at[k], y_peer)
        yield
    for k in ORDER:
        zz = lax.rem(z + k, 4)
        second_x[k].wait_recv()
        top = (
            part[top_rows(y), cols(zz, x)].astype(F32)
            + from_y[k, :, lane(x)].astype(F32)
            + late_x[k].astype(F32)
        )
        second_y[k].wait_recv()
        bottom = (
            part[low_rows(y), cols(zz, x)].astype(F32) + from_x[k, y].astype(F32) + late_y[k].astype(F32)
        )
        if k:
            to_z[k - 1, :cut] = top.astype(BF16)
            to_z[k - 1, cut:] = bottom.astype(BF16)
            third[k] = sender.send(to_z.at[k - 1], from_z.at[k - 1], z_peers[k - 1])
        else:
            total = jnp.concatenate([top, bottom], axis=0) + base[here].astype(F32)
        yield
    for k in (1, 2, 3):
        third[k].wait_recv()
    total = total + (from_z[0].astype(F32) + from_z[1].astype(F32) + from_z[2].astype(F32))
    mapped[here] = total
    low[here, cols(z, x)] = total.astype(BF16)
    own = low.at[here, cols(z, x)]
    to_line = [sender.send(own, own, peer) for peer in z_peers]
    over_x = [sender.send(own, own, x_peer)]
    yield
    for k in (1, 3, 2):
        to_line[k - 1].wait_recv()
        block = low.at[here, cols(lax.rem(z + 4 - k, 4), x)]
        over_x.append(sender.send(block, block, x_peer))
        yield
    for copy in over_x:
        copy.wait_recv()
    yield


MAP_SCHEDULE = [0] * 4 + [0, 1] * 8 + [0, 1, 1, 0, 1, 0, 1, 0, 1, 1, 1, 1, 1, 0]


def stream_columns(z, pairs, local_sem, width):
    loads = {}
    for k in ORDER:
        span = pl.ds(pl.multiple_of(lax.rem(z + k, 4) * width, width), width)
        loads[k] = [
            pltpu.make_async_copy(source.at[:, span], held.at[k], local_sem.at[i, k])
            for i, (source, held) in enumerate(pairs)
        ]
        for load in loads[k]:
            load.start()
    return loads


def map_kernel(left_own, left_other, weight_own, weight_other, base, mapped, low, *rest):
    part, held_own, held_other = rest[:3]
    scratch, (send_sem, recv_sem, local_sem) = rest[3:-3], rest[-3:]
    spot = place()
    loads = stream_columns(
        spot[0], ((weight_own, held_own), (weight_other, held_other)), local_sem, held_own.shape[2]
    )

    def fill(k, pair):
        for load in loads[k]:
            load.wait()
        part[:, pair] = (
            jnp.dot(left_own[...], held_own[k], preferred_element_type=F32)
            + jnp.dot(left_other[...], held_other[k], preferred_element_type=F32)
        ).astype(BF16)

    greet(spot[3] + list(spot[4:]))
    sender = Sender(send_sem, recv_sem)
    cut = scratch[2].shape[2]
    steps = [map_steps(c, sender, spot, cut, fill, part, base, mapped, low, *scratch) for c in range(CHUNKS)]
    interleave(steps[0], steps[1], MAP_SCHEDULE)
    sender.drain()


def reduce_map(lefts, weights, base):
    rows, width = base.shape
    span = rows // CHUNKS
    cut = span // 6 * 5
    return pl.pallas_call(
        map_kernel,
        out_shape=(
            jax.ShapeDtypeStruct((rows, width), F32),
            jax.ShapeDtypeStruct((rows, 8 * width), BF16),
        ),
        in_specs=[
            pl.BlockSpec(memory_space=pltpu.VMEM),
            pl.BlockSpec(memory_space=pltpu.VMEM),
            pl.BlockSpec(memory_space=pl.ANY),
            pl.BlockSpec(memory_space=pl.ANY),
            pl.BlockSpec(memory_space=pltpu.VMEM),
        ],
        out_specs=[pl.BlockSpec(memory_space=pltpu.VMEM)] * 2,
        scratch_shapes=[
            pltpu.VMEM((2 * rows, 8 * width), BF16),
            pltpu.VMEM((4, weights[0].shape[0], 2 * width), BF16),
            pltpu.VMEM((4, weights[1].shape[0], 2 * width), BF16),
            pltpu.VMEM((CHUNKS, 4, cut, 2 * width), BF16),
            pltpu.VMEM((CHUNKS, 4, 2, span - cut, width), BF16),
            pltpu.VMEM((CHUNKS, 4, cut, width), BF16),
            pltpu.VMEM((CHUNKS, 4, span - cut, width), BF16),
            pltpu.VMEM((CHUNKS, 4, cut, width), BF16),
            pltpu.VMEM((CHUNKS, 4, span - cut, width), BF16),
            pltpu.VMEM((CHUNKS, 3, span, width), BF16),
            pltpu.VMEM((CHUNKS, 3, span, width), BF16),
            pltpu.SemaphoreType.DMA((30 * CHUNKS,)),
            pltpu.SemaphoreType.DMA((30 * CHUNKS,)),
            pltpu.SemaphoreType.DMA((2, 4)),
        ],
        compiler_params=pltpu.CompilerParams(collective_id=2, has_side_effects=True),
    )(*lefts, *weights, base)


def dual_steps(chunk, sender, spot, fill, part, base, mapped, full, from_x, to_z, from_z):
    z, x, y, z_peers, x_peer, y_peer = spot
    rows, width = base.shape
    span = rows // CHUNKS
    cut = span // 6 * 5
    cols = lambda zz, xx: pl.ds(pl.multiple_of((zz * 2 + xx) * width, width), width)
    here = slice(chunk * span, (chunk + 1) * span)
    view = lambda zz, xx, yy: full.at[
        pl.ds(pl.multiple_of(yy * rows + chunk * span, 16), span), cols(zz, xx)
    ]
    top = lambda zz, xx, yy: full.at[pl.ds(pl.multiple_of(yy * rows + chunk * span, 16), cut), cols(zz, xx)]
    bottom = lambda zz, xx, yy: full.at[
        pl.ds(pl.multiple_of(yy * rows + chunk * span + cut, 16), span - cut), cols(zz, xx)
    ]
    from_x, to_z, from_z = (ref.at[chunk] for ref in (from_x, to_z, from_z))
    first, third = {}, {}
    for k in ORDER:
        if chunk == 0:
            fill(k, pl.ds(pl.multiple_of(lax.rem(z + k, 4) * 2 * width, 2 * width), 2 * width))
        first[k] = sender.send(part.at[here, cols(lax.rem(z + k, 4), 1 - x)], from_x.at[k], x_peer)
        yield
    for k in ORDER:
        first[k].wait_recv()
        total = part[here, cols(lax.rem(z + k, 4), x)].astype(F32) + from_x[k].astype(F32)
        if k:
            to_z[k - 1] = total.astype(BF16)
            third[k] = sender.send(to_z.at[k - 1], from_z.at[k - 1], z_peers[k - 1])
        yield
    for k in (1, 2, 3):
        third[k].wait_recv()
    grad = (mapped[here] + total) + (
        from_z[0].astype(F32) + from_z[1].astype(F32) + from_z[2].astype(F32)
    )
    full[pl.ds(pl.multiple_of(y * rows + chunk * span, 16), span), cols(z, x)] = (
        base[here].astype(F32) - grad
    ).astype(BF16)
    yield from gather_steps(sender, view, top, bottom, spot)


DUAL_SCHEDULE = [0] * 4 + [0, 1] * 4 + [0, 1, 0, 1, 0, 1, 0, 1, 1] + [0, 1] * 3 + [0] + [1] * 4 + [0, 1]


def dual_kernel(left, weight, base, mapped, full, part, held, from_x, to_z, from_z, send_sem, recv_sem, local_sem):
    spot = place()
    loads = stream_columns(spot[0], ((weight, held),), local_sem, held.shape[2])

    def fill(k, pair):
        loads[k][0].wait()
        part[:, pair] = jnp.dot(left[...], held[k], preferred_element_type=F32).astype(BF16)

    greet(spot[3] + list(spot[4:]))
    sender = Sender(send_sem, recv_sem)
    steps = [
        dual_steps(c, sender, spot, fill, part, base, mapped, full, from_x, to_z, from_z) for c in range(CHUNKS)
    ]
    interleave(steps[0], steps[1], DUAL_SCHEDULE)
    sender.drain()


def reduce_dual(left, weight, base, mapped):
    rows, width = base.shape
    span = rows // CHUNKS
    return pl.pallas_call(
        dual_kernel,
        out_shape=jax.ShapeDtypeStruct((2 * rows, weight.shape[1]), BF16),
        in_specs=[
            pl.BlockSpec(memory_space=pltpu.VMEM),
            pl.BlockSpec(memory_space=pl.ANY),
            pl.BlockSpec(memory_space=pltpu.VMEM),
            pl.BlockSpec(memory_space=pltpu.VMEM),
        ],
        out_specs=pl.BlockSpec(memory_space=pltpu.VMEM),
        scratch_shapes=[
            pltpu.VMEM((rows, 8 * width), BF16),
            pltpu.VMEM((4, weight.shape[0], 2 * width), BF16),
            pltpu.VMEM((CHUNKS, 4, span, width), BF16),
            pltpu.VMEM((CHUNKS, 3, span, width), BF16),
            pltpu.VMEM((CHUNKS, 3, span, width), BF16),
            pltpu.SemaphoreType.DMA((26 * CHUNKS,)),
            pltpu.SemaphoreType.DMA((26 * CHUNKS,)),
            pltpu.SemaphoreType.DMA((1, 4)),
        ],
        compiler_params=pltpu.CompilerParams(collective_id=3, has_side_effects=True),
    )(left, weight, base, mapped)


def chip_body(
    samples,
    dual_weight,
    dual_vector,
    map_weight,
    map_vector,
    moment_weight,
    square_weight,
    moment_vector,
    square_vector,
):
    swap = [(0, 1), (1, 0), (2, 3), (3, 2)]
    fsdp, rep = lax.axis_index("fsdp"), lax.axis_index("rep")
    vector = map_vector.astype(BF16)
    vectors = (vector, lax.ppermute(vector, "rep", swap))
    rows, weights = gather_samples(samples, map_weight)
    inverse_rows = 1.0 / (rows.shape[0] * 2)
    sigmas, scales = [], []
    for block, pair in zip(weights, vectors):
        sigma = jax.nn.sigmoid(contract_last(rows, block) + pair[1].astype(F32))
        sigmas.append(sigma)
        scales.append((pair[0].astype(F32) * sigma).astype(BF16))
    half, width = rows.shape[0] // 2, rows.shape[1] // 8
    base = lax.dynamic_slice(rows, ((rep // 2) * half, fsdp * width), (half, width))
    mapped, mapped_low = reduce_map(scales, weights, base)
    dual_hidden = contract_last(mapped_low, dual_weight) + dual_vector[1]
    dual_scaled = (dual_vector[0] * jax.nn.sigmoid(dual_hidden)).astype(BF16)
    residual = reduce_dual(dual_scaled, dual_weight, base, mapped)
    grads, smalls = [], []
    for block, pair, sigma, scaled in zip(weights[::-1], vectors[::-1], sigmas[::-1], scales[::-1]):
        readout = pair[0].astype(F32)
        pulled = contract_last(residual, block)
        curve = readout * (sigma * (1.0 - sigma)) * pulled
        grads.append(contract_first(scaled, residual) + contract_first(curve.astype(BF16), rows))
        smalls.append(jnp.stack([jnp.sum(sigma * pulled, axis=0), jnp.sum(curve, axis=0)]))
    owner_weight = (grads[1] + lax.ppermute(grads[0], "rep", swap)) * inverse_rows
    owner_vector = (smalls[1] + lax.ppermute(smalls[0], "rep", swap)) * inverse_rows
    next_weight, next_moment_weight, next_square_weight = adam_update(
        map_weight, owner_weight, moment_weight, square_weight
    )
    raw_vector, next_moment_vector, next_square_vector = adam_update(
        map_vector, owner_vector, moment_vector, square_vector
    )
    next_vector = jnp.concatenate([jnp.maximum(raw_vector[0:1], 0.0), raw_vector[1:2]], axis=0)
    return (
        next_weight,
        next_vector,
        next_moment_weight,
        next_square_weight,
        next_moment_vector,
        next_square_vector,
    )


def body(
    samples,
    dual_weight,
    dual_vector,
    map_weight,
    map_vector,
    moment_weight,
    square_weight,
    moment_vector,
    square_vector,
):
    group_rows = lax.all_gather(samples, "fsdp", axis=0, tiled=True)
    weight_slab, vector_slab = (
        lax.all_gather(map_weight.astype(jnp.bfloat16), "rep", axis=0, tiled=True),
        lax.all_gather(map_vector.astype(jnp.bfloat16), "rep", axis=1, tiled=True),
    )
    readout = vector_slab[0].astype(jnp.float32)
    offset = vector_slab[1].astype(jnp.float32)
    inverse_rows = 1.0 / (group_rows.shape[0] * lax.axis_size("rep"))
    hidden = contract_last(group_rows, weight_slab) + offset
    sigma = jax.nn.sigmoid(hidden)
    scaled = (readout * sigma).astype(jnp.bfloat16)
    group_float = group_rows.astype(jnp.float32)
    mapped = group_float + lax.psum(
        jnp.dot(scaled, weight_slab, preferred_element_type=jnp.float32).astype(jnp.bfloat16),
        "fsdp",
    ).astype(jnp.float32)
    mapped_low = mapped.astype(jnp.bfloat16)
    dual_hidden = contract_last(mapped_low, dual_weight) + dual_vector[1]
    dual_scaled = (dual_vector[0] * jax.nn.sigmoid(dual_hidden)).astype(jnp.bfloat16)
    dual_grad = mapped + lax.psum(
        jnp.dot(dual_scaled, dual_weight, preferred_element_type=jnp.float32).astype(jnp.bfloat16),
        "fsdp",
    ).astype(jnp.float32)
    residual = (group_float - dual_grad).astype(jnp.bfloat16)
    pulled = contract_last(residual, weight_slab)
    slope = sigma * (1.0 - sigma)
    curve_float = readout * slope * pulled
    curve_term = curve_float.astype(jnp.bfloat16)
    left_stack = jnp.concatenate([scaled, curve_term], axis=0)
    right_stack = jnp.concatenate([residual, group_rows], axis=0)
    grad_slab = contract_first(left_stack, right_stack) * inverse_rows
    grad_small = (
        jnp.stack([jnp.sum(sigma * pulled, axis=0), jnp.sum(curve_float, axis=0)]) * inverse_rows
    )
    owner_weight, owner_vector = (
        lax.psum_scatter(grad_slab, "rep", scatter_dimension=0, tiled=True),
        lax.psum_scatter(grad_small, "rep", scatter_dimension=1, tiled=True),
    )
    next_weight, next_moment_weight, next_square_weight = adam_update(
        map_weight, owner_weight, moment_weight, square_weight
    )
    raw_vector, next_moment_vector, next_square_vector = adam_update(
        map_vector, owner_vector, moment_vector, square_vector
    )
    next_vector = jnp.concatenate([jnp.maximum(raw_vector[0:1], 0.0), raw_vector[1:2]], axis=0)
    return (
        next_weight,
        next_vector,
        next_moment_weight,
        next_square_weight,
        next_moment_vector,
        next_square_vector,
    )


def solution(mesh):
    by_chip = mesh.shape["fsdp"] == 8 and mesh.shape["rep"] == 4
    return jax.shard_map(
        chip_body if by_chip else body,
        mesh=mesh,
        in_specs=(
            P(("fsdp", "rep"), None),
            P("fsdp", None),
            P(None, "fsdp"),
            P(("fsdp", "rep"), None),
            P(None, ("fsdp", "rep")),
            P(("fsdp", "rep"), None),
            P(("fsdp", "rep"), None),
            P(None, ("fsdp", "rep")),
            P(None, ("fsdp", "rep")),
        ),
        out_specs=(
            P(("fsdp", "rep"), None),
            P(None, ("fsdp", "rep")),
            P(("fsdp", "rep"), None),
            P(("fsdp", "rep"), None),
            P(None, ("fsdp", "rep")),
            P(None, ("fsdp", "rep")),
        ),
        check_vma=False,
    )
```
